32 devices in a mesh: lon: 8 (over z, x), lat: 4 (over y, core).
Axes of the slice: x: 2, y: 2, z: 4, core: 2. Of those that a mesh axis runs over, the one named last changes fastest.
Arguments:
- grid_field: float32 [4, 64, 16, 2048], P(None, 'lat', None, 'lon'), may hold values from -6 to 6
- lat_weight: float32 [64], replicated, may hold values from 0.3 to 3
Outputs:
- spec_real: float32 [4, 64, 16, 1024], P(None, None, 'lat', 'lon')
- spec_imag: float32 [4, 64, 16, 1024], P(None, None, 'lat', 'lon')
The draws below stay inside these ranges and needn't reach their ends.
All inputs are finite; a program needn't handle non-finite values.
Results may differ from the reference program's by a relative error of at most 0.000071.
Values sent between devices are 32-bit elements; how exact they have to be, the bound alone decides.
A program may use at most 64 MiB of HBM per device.

```python
import math
import jax
import jax.numpy as jnp

NLON = 2048
MODES = 1024
F = 4
R = 16
NLAT = 64


def shard_levels(key, dims, shards, smallest, high):
    def one(position, parts):
        steps = jax.random.uniform(jax.random.fold_in(jax.random.fold_in(key, 6), position), (parts,), jnp.float32, smallest / len(shards), high / len(shards))
        return jnp.repeat(jnp.exp(steps), dims[position] // parts).reshape((-1,) + (1,) * (len(dims) - position - 1))

    factor_of = one(*shards[0])
    for cut in shards[1:]:
        factor_of = factor_of * one(*cut)
    return factor_of


def scatter_about(stream_key, shape, scale, limit, cuts=(), dtype=jnp.bfloat16):
    array = scale * jax.random.normal(stream_key, shape, jnp.float32)
    if cuts:
        array = array * shard_levels(stream_key, shape, cuts, -0.22, 0.18)
    return jnp.clip(array, -limit, limit).astype(dtype)


def setup_inputs(seed: int = 0) -> dict:
    seeds = jax.random.split(jax.random.key(seed), 3)
    grid_field = scatter_about(seeds[0], (F, NLAT, R, NLON), 1.0, 6.0, ((1, 4), (3, 8)), jnp.float32)
    lat_weight = jnp.clip(jnp.exp(jax.random.uniform(seeds[1], (NLAT,), jnp.float32, math.log(0.3), math.log(3.0))), 0.3, 3.0)
    return dict(grid_field=grid_field, lat_weight=lat_weight)


def reference(grid_field, lat_weight):
    normalizer = 1.0 / math.sqrt(NLON)
    spectra = jnp.fft.rfft(grid_field, axis=-1)[..., :MODES] * normalizer
    weights_row = lat_weight[None, :, None, None]
    spec_real = (jnp.real(spectra) * weights_row).astype(jnp.float32)
    spec_imag = (jnp.imag(spectra) * weights_row).astype(jnp.float32)
    return (spec_real, spec_imag)
```

```python
import functools
import math

import jax
import jax.numpy as jnp
import numpy as np
from jax import lax
from jax.experimental import pallas as pl
from jax.experimental.pallas import tpu as pltpu
from jax.sharding import PartitionSpec as P

MODES = 1024
CHUNKS = 4
LANES = 128
MESH = pl.DeviceIdType.MESH


def tables(cycle, lon_dev, width):
    length = cycle * lon_dev
    j = np.arange(lon_dev, dtype=np.int64)
    phase = np.arange(cycle)[:, None] * j[None, :] % length * (2.0 * math.pi / length)
    twiddle = np.stack([np.cos(phase), -np.sin(phase)]).astype(np.float32)
    phase = j[:, None] * np.arange(width)[None, :] % lon_dev * (2.0 * math.pi / lon_dev)
    real, imag = np.cos(phase) / math.sqrt(length), -np.sin(phase) / math.sqrt(length)
    dft = np.block([[real, imag], [-imag, real]]).astype(np.float32)
    high = dft.astype(jnp.bfloat16)
    low = (dft - high.astype(np.float32)).astype(jnp.bfloat16)
    return twiddle, np.stack([high, low])


def kernel(
    cycle, groups, chunks, part, lat_dev, mode_dev,
    x_ref, weight_ref, twiddle_hbm, dft_hbm, out_ref,
    held, stage, twiddle, dft, b_high, b_low,
    table_sem, send_sem, held_sem, stage_sem, out_sem,
):
    lon, lat = lax.axis_index("lon"), lax.axis_index("lat")
    me = lon * groups + lat
    everyone = cycle * groups
    rows_dev = chunks * part
    radii, lon_dev = x_ref.shape[1], x_ref.shape[2]
    radii_dev = radii // groups
    rows = part * radii
    width = dft.shape[2] // 2

    table_copies = [
        pltpu.make_async_copy(twiddle_hbm, twiddle, table_sem.at[0]),
        pltpu.make_async_copy(dft_hbm, dft, table_sem.at[1]),
    ]
    for copy in table_copies:
        copy.start()

    def own(c):
        return pltpu.make_async_copy(
            x_ref.at[pl.ds(lon * rows_dev + c * part, part)], held.at[c, lon], held_sem.at[c]
        )

    for c in range(chunks):
        own(c).start()

    barrier = pltpu.get_barrier_semaphore()

    @pl.loop(1, everyone)
    def _(i):
        peer = lax.rem(me + i, everyone)
        pl.semaphore_signal(
            barrier, inc=1, device_id={"lon": peer // groups, "lat": lax.rem(peer, groups)},
            device_id_type=MESH,
        )

    pl.semaphore_wait(barrier, everyone - 1)

    for c in range(chunks):
        for i in range(1, cycle):
            peer = lax.rem(lon + i, cycle)
            pltpu.make_async_remote_copy(
                src_ref=x_ref.at[pl.ds(peer * rows_dev + c * part, part)],
                dst_ref=held.at[c, lon],
                send_sem=send_sem,
                recv_sem=held_sem.at[c],
                device_id={"lon": peer},
                device_id_type=MESH,
            ).start()

    for copy in table_copies:
        copy.wait()

    lane = lax.broadcasted_iota(jnp.int32, (rows, width), 1)
    residue = lax.rem(lane, cycle)
    step = lane // cycle

    def chunk(c, carry):
        pltpu.make_async_copy(held.at[c], held.at[c], held_sem.at[c]).wait()
        blocks = [held[c, l].reshape(rows, lon_dev) for l in range(cycle)]
        for s in range(cycle // 2 + 1):
            real = imag = None
            for l in range(cycle):
                angle = 2.0 * math.pi * (l * s % cycle) / cycle
                co, si = math.cos(angle), -math.sin(angle)
                if abs(co) > 1e-9:
                    term = blocks[l] * np.float32(co)
                    real = term if real is None else real + term
                if abs(si) > 1e-9:
                    term = blocks[l] * np.float32(si)
                    imag = term if imag is None else imag + term
            for t in sorted({s, (cycle - s) % cycle}):
                sign = 1.0 if t == s else -1.0
                tr, ti = twiddle[0, t:t + 1, :], twiddle[1, t:t + 1, :]
                if imag is None:
                    re, im = real * tr, real * ti
                else:
                    re = real * tr - imag * (ti * sign)
                    im = real * ti + imag * (tr * sign)
                for part_of, at in ((re, 0), (im, lon_dev)):
                    high = part_of.astype(jnp.bfloat16)
                    b_high[t * rows:(t + 1) * rows, at:at + lon_dev] = high
                    b_low[t * rows:(t + 1) * rows, at:at + lon_dev] = (
                        part_of - high.astype(jnp.float32)
                    ).astype(jnp.bfloat16)
        dot = functools.partial(jnp.dot, preferred_element_type=jnp.float32)
        z = dot(b_high[...], dft[0]) + dot(b_low[...], dft[0]) + dot(b_high[...], dft[1])
        first = lon * rows_dev + c * part
        time = lat * lat_dev + lax.rem(first, lat_dev)
        scale = [weight_ref[time + p] for p in range(part)]
        for owner in range(cycle):
            index = step + owner * (mode_dev // cycle)
            index = jnp.minimum(index, width - 1)
            for half in range(2):
                value = None
                for s in range(cycle):
                    piece = jnp.take_along_axis(
                        z[s * rows:(s + 1) * rows, half * width:(half + 1) * width],
                        index, axis=1, mode="promise_in_bounds",
                    )
                    value = piece if value is None else jnp.where(residue == s, piece, value)
                for p in range(part):
                    scaled = value[p * radii:(p + 1) * radii] * scale[p]
                    for g in range(groups):
                        stage[c, owner * groups + g, half, p] = scaled[
                            g * radii_dev:(g + 1) * radii_dev, :mode_dev
                        ]
        field = first // lat_dev
        target = out_ref.at[:, field, pl.ds(time, part)]
        pltpu.make_async_copy(stage.at[c, me], target, out_sem).start()

        @pl.loop(1, everyone)
        def _(i):
            peer = lax.rem(me + i, everyone)
            pltpu.make_async_remote_copy(
                src_ref=stage.at[c, peer],
                dst_ref=target,
                send_sem=stage_sem,
                recv_sem=out_sem,
                device_id={"lon": peer // groups, "lat": lax.rem(peer, groups)},
                device_id_type=MESH,
            ).start()

        return carry

    lax.fori_loop(0, chunks, chunk, 0)

    sent = x_ref.at[pl.ds(0, (cycle - 1) * rows_dev)]
    pltpu.make_async_copy(sent, sent, send_sem).wait()
    for c in range(chunks):
        staged = stage.at[c, pl.ds(0, everyone - 1)]
        pltpu.make_async_copy(staged, staged, stage_sem).wait()
    pltpu.make_async_copy(out_ref, out_ref, out_sem).wait()


def per_device(grid_field, lat_weight):
    fields, lat_dev, radii, lon_dev = grid_field.shape
    cycle, groups = lax.axis_size("lon"), lax.axis_size("lat")
    mode_dev = MODES // cycle
    width = -(-mode_dev // LANES) * LANES
    rows_dev = fields * lat_dev // cycle
    part = max(1, rows_dev // CHUNKS)
    chunks = rows_dev // part
    rows = part * radii
    twiddle, dft = tables(cycle, lon_dev, width)
    out = pl.pallas_call(
        functools.partial(kernel, cycle, groups, chunks, part, lat_dev, mode_dev),
        out_shape=jax.ShapeDtypeStruct(
            (2, fields, lat_dev * groups, radii // groups, mode_dev), jnp.float32
        ),
        in_specs=[
            pl.BlockSpec(memory_space=pl.ANY),
            pl.BlockSpec(memory_space=pltpu.SMEM),
            pl.BlockSpec(memory_space=pl.ANY),
            pl.BlockSpec(memory_space=pl.ANY),
        ],
        out_specs=pl.BlockSpec(memory_space=pltpu.VMEM),
        scratch_shapes=[
            pltpu.VMEM((chunks, cycle, part, radii, lon_dev), jnp.float32),
            pltpu.VMEM((chunks, cycle * groups, 2, part, radii // groups, mode_dev), jnp.float32),
            pltpu.VMEM(twiddle.shape, jnp.float32),
            pltpu.VMEM(dft.shape, jnp.bfloat16),
            pltpu.VMEM((cycle * rows, 2 * lon_dev), jnp.bfloat16),
            pltpu.VMEM((cycle * rows, 2 * lon_dev), jnp.bfloat16),
            pltpu.SemaphoreType.DMA((2,)),
            pltpu.SemaphoreType.DMA,
            pltpu.SemaphoreType.DMA((chunks,)),
            pltpu.SemaphoreType.DMA,
            pltpu.SemaphoreType.DMA,
        ],
        compiler_params=pltpu.CompilerParams(collective_id=0, has_side_effects=True),
    )(
        grid_field.reshape(fields * lat_dev, radii, lon_dev), lat_weight,
        jnp.asarray(twiddle), jnp.asarray(dft),
    )
    return out[0], out[1]


def solution(mesh):
    in_specs = (P(None, "lat", None, "lon"), P())
    out_specs = (P(None, None, "lat", "lon"), P(None, None, "lat", "lon"))
    return jax.shard_map(
        per_device, mesh=mesh, in_specs=in_specs, out_specs=out_specs, check_vma=False
    )
```

```python
import functools
import math

import jax
import jax.numpy as jnp
import numpy as np
from jax import lax
from jax.experimental import pallas as pl
from jax.experimental.pallas import tpu as pltpu
from jax.sharding import PartitionSpec as P

MODES = 1024
CHUNKS = 4
LANES = 128
MESH = pl.DeviceIdType.MESH


def tables(cycle, lon_dev, width):
    length = cycle * lon_dev
    j = np.arange(lon_dev, dtype=np.int64)
    phase = np.arange(cycle)[:, None] * j[None, :] % length * (2.0 * math.pi / length)
    twiddle = np.stack([np.cos(phase), -np.sin(phase)]).astype(np.float32)
    phase = j[:, None] * np.arange(width)[None, :] % lon_dev * (2.0 * math.pi / lon_dev)
    real, imag = np.cos(phase) / math.sqrt(length), -np.sin(phase) / math.sqrt(length)
    dft = np.block([[real, imag], [-imag, real]]).astype(np.float32)
    high = dft.astype(jnp.bfloat16)
    low = (dft - high.astype(np.float32)).astype(jnp.bfloat16)
    return twiddle, np.stack([high, low])


def kernel(
    cycle, groups, chunks, part, lat_dev, mode_dev,
    x_ref, weight_hbm, twiddle_hbm, dft_hbm, out_ref,
    held, stage, twiddle, dft, b_high, b_low,
    weight_ref, flood_sem, table_sem, send_sem, held_sem, stage_sem, out_sem,
):
    lon, lat = lax.axis_index("lon"), lax.axis_index("lat")
    me = lon * groups + lat
    everyone = cycle * groups
    rows_dev = chunks * part
    radii, lon_dev = x_ref.shape[1], x_ref.shape[2]
    radii_dev = radii // groups
    rows = part * radii
    width = dft.shape[2] // 2

    table_copies = [
        pltpu.make_async_copy(twiddle_hbm, twiddle, table_sem.at[0]),
        pltpu.make_async_copy(dft_hbm, dft, table_sem.at[1]),
        pltpu.make_async_copy(weight_hbm, weight_ref, table_sem.at[2]),
    ]
    for copy in table_copies:
        copy.start()

    def own(c):
        return pltpu.make_async_copy(
            x_ref.at[pl.ds(lon * rows_dev + c * part, part)], held.at[c, lon], held_sem.at[c]
        )

    for c in range(chunks):
        own(c).start()

    def send(c, peer):
        pltpu.make_async_remote_copy(
            src_ref=x_ref.at[pl.ds(peer * rows_dev + c * part, part)],
            dst_ref=held.at[c, lon],
            send_sem=send_sem,
            recv_sem=held_sem.at[c],
            device_id={"lon": peer},
            device_id_type=MESH,
        ).start()

    lon_row, lon_side = lon // 2, lax.rem(lon, 2)
    lat_row, lat_side = lat // 2, lax.rem(lat, 2)
    neighbours = [
        (lon_row > 0, lon - 2, lat),
        (lon_row < cycle // 2 - 1, lon + 2, lat),
        (lon_side >= 0, lon + 1 - 2 * lon_side, lat),
        (lat_row > 0, lon, lat - 2),
        (lat_row < groups // 2 - 1, lon, lat + 2),
        (lat_side >= 0, lon, lat + 1 - 2 * lat_side),
    ]

    def flood(sem):
        for present, to_lon, to_lat in neighbours:
            @pl.when(present)
            def _():
                pl.semaphore_signal(
                    sem, inc=1, device_id={"lon": to_lon, "lat": to_lat}, device_id_type=MESH
                )
        pl.semaphore_wait(sem, sum(jnp.where(present, 1, 0) for present, _, _ in neighbours))

    for r in range(1, cycle // 2 + 1):
        flood(pltpu.get_barrier_semaphore() if r == 1 else flood_sem.at[r - 2])
        for step, side in ((r, lon_side), (r - 1, 1 - lon_side)):
            for way in ((1, -1) if step else (1,)):
                row = lon_row + way * step

                @pl.when((row >= 0) & (row < cycle // 2))
                def _():
                    send(0, 2 * row + side)

    for c in range(1, chunks):
        for i in range(1, cycle):
            send(c, lax.rem(lon + i, cycle))

    for r in range(cycle // 2 + 1, cycle // 2 + groups // 2 + 1):
        flood(flood_sem.at[r - 2])

    for copy in table_copies:
        copy.wait()

    lane = lax.broadcasted_iota(jnp.int32, (rows, width), 1)
    residue = lax.rem(lane, cycle)
    step = lane // cycle

    def chunk(c, carry):
        pltpu.make_async_copy(held.at[c], held.at[c], held_sem.at[c]).wait()
        blocks = [held[c, l].reshape(rows, lon_dev) for l in range(cycle)]
        for s in range(cycle // 2 + 1):
            real = imag = None
            for l in range(cycle):
                angle = 2.0 * math.pi * (l * s % cycle) / cycle
                co, si = math.cos(angle), -math.sin(angle)
                if abs(co) > 1e-9:
                    term = blocks[l] * np.float32(co)
                    real = term if real is None else real + term
                if abs(si) > 1e-9:
                    term = blocks[l] * np.float32(si)
                    imag = term if imag is None else imag + term
            for t in sorted({s, (cycle - s) % cycle}):
                sign = 1.0 if t == s else -1.0
                tr, ti = twiddle[0, t:t + 1, :], twiddle[1, t:t + 1, :]
                if imag is None:
                    re, im = real * tr, real * ti
                else:
                    re = real * tr - imag * (ti * sign)
                    im = real * ti + imag * (tr * sign)
                for part_of, at in ((re, 0), (im, lon_dev)):
                    high = part_of.astype(jnp.bfloat16)
                    b_high[t * rows:(t + 1) * rows, at:at + lon_dev] = high
                    b_low[t * rows:(t + 1) * rows, at:at + lon_dev] = (
                        part_of - high.astype(jnp.float32)
                    ).astype(jnp.bfloat16)
        dot = functools.partial(jnp.dot, preferred_element_type=jnp.float32)
        z = dot(b_high[...], dft[0]) + dot(b_low[...], dft[0]) + dot(b_high[...], dft[1])
        first = lon * rows_dev + c * part
        time = lat * lat_dev + lax.rem(first, lat_dev)
        scale = [weight_ref[time + p] for p in range(part)]
        for owner in range(cycle):
            index = step + owner * (mode_dev // cycle)
            index = jnp.minimum(index, width - 1)
            for half in range(2):
                value = None
                for s in range(cycle):
                    piece = jnp.take_along_axis(
                        z[s * rows:(s + 1) * rows, half * width:(half + 1) * width],
                        index, axis=1, mode="promise_in_bounds",
                    )
                    value = piece if value is None else jnp.where(residue == s, piece, value)
                for p in range(part):
                    scaled = value[p * radii:(p + 1) * radii] * scale[p]
                    for g in range(groups):
                        stage[c, owner * groups + g, half, p] = scaled[
                            g * radii_dev:(g + 1) * radii_dev, :mode_dev
                        ]
        field = first // lat_dev
        target = out_ref.at[:, field, pl.ds(time, part)]
        pltpu.make_async_copy(stage.at[c, me], target, out_sem).start()

        @pl.loop(1, everyone)
        def _(i):
            peer = lax.rem(me + i, everyone)
            pltpu.make_async_remote_copy(
                src_ref=stage.at[c, peer],
                dst_ref=target,
                send_sem=stage_sem,
                recv_sem=out_sem,
                device_id={"lon": peer // groups, "lat": lax.rem(peer, groups)},
                device_id_type=MESH,
            ).start()

        return carry

    lax.fori_loop(0, chunks, chunk, 0)

    sent = x_ref.at[pl.ds(0, (cycle - 1) * rows_dev)]
    pltpu.make_async_copy(sent, sent, send_sem).wait()
    for c in range(chunks):
        staged = stage.at[c, pl.ds(0, everyone - 1)]
        pltpu.make_async_copy(staged, staged, stage_sem).wait()
    pltpu.make_async_copy(out_ref, out_ref, out_sem).wait()


def split(both_ref, real_ref, imag_ref, sem):
    copies = [
        pltpu.make_async_copy(both_ref.at[i, f], ref.at[f], sem.at[i, f])
        for i, ref in enumerate((real_ref, imag_ref)) for f in range(ref.shape[0])
    ]
    for copy in copies:
        copy.start()
    for copy in copies:
        copy.wait()


def per_device(grid_field, lat_weight):
    fields, lat_dev, radii, lon_dev = grid_field.shape
    cycle, groups = lax.axis_size("lon"), lax.axis_size("lat")
    mode_dev = MODES // cycle
    width = -(-mode_dev // LANES) * LANES
    rows_dev = fields * lat_dev // cycle
    part = max(1, rows_dev // CHUNKS)
    chunks = rows_dev // part
    rows = part * radii
    twiddle, dft = tables(cycle, lon_dev, width)
    out = pl.pallas_call(
        functools.partial(kernel, cycle, groups, chunks, part, lat_dev, mode_dev),
        out_shape=pltpu.VMEM(
            (2, fields, lat_dev * groups, radii // groups, mode_dev), jnp.float32
        ),
        in_specs=[
            pl.BlockSpec(memory_space=pl.ANY),
            pl.BlockSpec(memory_space=pl.ANY),
            pl.BlockSpec(memory_space=pl.ANY),
            pl.BlockSpec(memory_space=pl.ANY),
        ],
        out_specs=pl.BlockSpec(memory_space=pltpu.VMEM),
        scratch_shapes=[
            pltpu.VMEM((chunks, cycle, part, radii, lon_dev), jnp.float32),
            pltpu.VMEM((chunks, cycle * groups, 2, part, radii // groups, mode_dev), jnp.float32),
            pltpu.VMEM(twiddle.shape, jnp.float32),
            pltpu.VMEM(dft.shape, jnp.bfloat16),
            pltpu.VMEM((cycle * rows, 2 * lon_dev), jnp.bfloat16),
            pltpu.VMEM((cycle * rows, 2 * lon_dev), jnp.bfloat16),
            pltpu.SMEM(lat_weight.shape, jnp.float32),
            pltpu.SemaphoreType.REGULAR((cycle // 2 + groups // 2 - 1,)),
            pltpu.SemaphoreType.DMA((3,)),
            pltpu.SemaphoreType.DMA,
            pltpu.SemaphoreType.DMA((chunks,)),
            pltpu.SemaphoreType.DMA,
            pltpu.SemaphoreType.DMA,
        ],
        compiler_params=pltpu.CompilerParams(collective_id=0, has_side_effects=True, vmem_limit_bytes=67_043_328 - 5 * 2**18),
    )(
        grid_field.reshape(fields * lat_dev, radii, lon_dev), lat_weight,
        jnp.asarray(twiddle), jnp.asarray(dft),
    )
    half = jax.ShapeDtypeStruct(out.shape[1:], jnp.float32)
    return pl.pallas_call(
        split,
        out_shape=(half, half),
        in_specs=[pl.BlockSpec(memory_space=pltpu.VMEM)],
        out_specs=(pl.BlockSpec(memory_space=pl.ANY), pl.BlockSpec(memory_space=pl.ANY)),
        scratch_shapes=[pltpu.SemaphoreType.DMA((2, fields))],
        compiler_params=pltpu.CompilerParams(vmem_limit_bytes=16 * 2**20),
    )(out)


def solution(mesh):
    in_specs = (P(None, "lat", None, "lon"), P())
    out_specs = (P(None, None, "lat", "lon"), P(None, None, "lat", "lon"))
    return jax.shard_map(
        per_device, mesh=mesh, in_specs=in_specs, out_specs=out_specs, check_vma=False
    )
```

```python
import functools
import math

import jax
import jax.numpy as jnp
import numpy as np
from jax import lax
from jax.experimental import pallas as pl
from jax.experimental.pallas import tpu as pltpu
from jax.sharding import PartitionSpec as P

MODES = 1024
CHUNKS = 2
LANES = 128
MESH = pl.DeviceIdType.MESH


def tables(cycle, lon_dev, width):
    length = cycle * lon_dev
    j = np.arange(lon_dev, dtype=np.int64)
    phase = np.arange(cycle)[:, None] * j[None, :] % length * (2.0 * math.pi / length)
    twiddle = np.stack([np.cos(phase), -np.sin(phase)]).astype(np.float32)
    phase = j[:, None] * np.arange(width)[None, :] % lon_dev * (2.0 * math.pi / lon_dev)
    real, imag = np.cos(phase) / math.sqrt(length), -np.sin(phase) / math.sqrt(length)
    dft = np.block([[real, imag], [-imag, real]]).astype(np.float32)
    high = dft.astype(jnp.bfloat16)
    low = (dft - high.astype(np.float32)).astype(jnp.bfloat16)
    return twiddle, np.stack([high, low])


def kernel(
    cycle, groups, chunks, part, lat_dev, mode_dev,
    x_ref, weight_hbm, twiddle_hbm, dft_hbm, out_ref,
    held, stage, twiddle, dft, b_high, b_low,
    weight_ref, flood_sem, table_sem, send_sem, held_sem, stage_sem, out_sem,
):
    lon, lat = lax.axis_index("lon"), lax.axis_index("lat")
    me = lon * groups + lat
    everyone = cycle * groups
    rows_dev = chunks * part
    radii, lon_dev = x_ref.shape[1], x_ref.shape[2]
    radii_dev = radii // groups
    rows = part * radii
    width = dft.shape[2] // 2

    table_copies = [
        pltpu.make_async_copy(twiddle_hbm, twiddle, table_sem.at[0]),
        pltpu.make_async_copy(dft_hbm, dft, table_sem.at[1]),
        pltpu.make_async_copy(weight_hbm, weight_ref, table_sem.at[2]),
    ]
    for copy in table_copies:
        copy.start()

    def own(c):
        return pltpu.make_async_copy(
            x_ref.at[pl.ds(lon * rows_dev + c * part, part)], held.at[c, lon], held_sem.at[c]
        )

    for c in range(chunks):
        own(c).start()

    def send(c, peer):
        pltpu.make_async_remote_copy(
            src_ref=x_ref.at[pl.ds(peer * rows_dev + c * part, part)],
            dst_ref=held.at[c, lon],
            send_sem=send_sem,
            recv_sem=held_sem.at[c],
            device_id={"lon": peer},
            device_id_type=MESH,
        ).start()

    lon_row, lon_side = lon // 2, lax.rem(lon, 2)
    lat_row, lat_side = lat // 2, lax.rem(lat, 2)
    neighbours = [
        (lon_row > 0, lon - 2, lat),
        (lon_row < cycle // 2 - 1, lon + 2, lat),
        (lon_side >= 0, lon + 1 - 2 * lon_side, lat),
        (lat_row > 0, lon, lat - 2),
        (lat_row < groups // 2 - 1, lon, lat + 2),
        (lat_side >= 0, lon, lat + 1 - 2 * lat_side),
    ]

    def flood(sem):
        for present, to_lon, to_lat in neighbours:
            @pl.when(present)
            def _():
                pl.semaphore_signal(
                    sem, inc=1, device_id={"lon": to_lon, "lat": to_lat}, device_id_type=MESH
                )
        pl.semaphore_wait(sem, sum(jnp.where(present, 1, 0) for present, _, _ in neighbours))

    for r in range(1, cycle // 2 + 1):
        flood(pltpu.get_barrier_semaphore() if r == 1 else flood_sem.at[r - 2])
        for step, side in ((r, lon_side), (r - 1, 1 - lon_side)):
            for way in ((1, -1) if step else (1,)):
                row = lon_row + way * step

                @pl.when((row >= 0) & (row < cycle // 2))
                def _():
                    send(0, 2 * row + side)

    for c in range(1, chunks):
        for i in range(1, cycle):
            send(c, lax.rem(lon + i, cycle))

    for r in range(cycle // 2 + 1, cycle // 2 + groups // 2 + 1):
        flood(flood_sem.at[r - 2])

    for copy in table_copies:
        copy.wait()

    lane = lax.broadcasted_iota(jnp.int32, (rows, width), 1)
    residue = lax.rem(lane, cycle)
    step = lane // cycle

    def chunk(c, carry):
        pltpu.make_async_copy(held.at[c], held.at[c], held_sem.at[c]).wait()
        blocks = [held[c, l].reshape(rows, lon_dev) for l in range(cycle)]
        for s in range(cycle // 2 + 1):
            real = imag = None
            for l in range(cycle):
                angle = 2.0 * math.pi * (l * s % cycle) / cycle
                co, si = math.cos(angle), -math.sin(angle)
                if abs(co) > 1e-9:
                    term = blocks[l] * np.float32(co)
                    real = term if real is None else real + term
                if abs(si) > 1e-9:
                    term = blocks[l] * np.float32(si)
                    imag = term if imag is None else imag + term
            for t in sorted({s, (cycle - s) % cycle}):
                sign = 1.0 if t == s else -1.0
                tr, ti = twiddle[0, t:t + 1, :], twiddle[1, t:t + 1, :]
                if imag is None:
                    re, im = real * tr, real * ti
                else:
                    re = real * tr - imag * (ti * sign)
                    im = real * ti + imag * (tr * sign)
                for part_of, at in ((re, 0), (im, lon_dev)):
                    high = part_of.astype(jnp.bfloat16)
                    b_high[t * rows:(t + 1) * rows, at:at + lon_dev] = high
                    b_low[t * rows:(t + 1) * rows, at:at + lon_dev] = (
                        part_of - high.astype(jnp.float32)
                    ).astype(jnp.bfloat16)
        dot = functools.partial(jnp.dot, preferred_element_type=jnp.float32)
        z = dot(b_high[...], dft[0]) + dot(b_low[...], dft[0]) + dot(b_high[...], dft[1])
        first = lon * rows_dev + c * part
        time = lat * lat_dev + lax.rem(first, lat_dev)
        scale = [weight_ref[time + p] for p in range(part)]
        for owner in range(cycle):
            index = step + owner * (mode_dev // cycle)
            index = jnp.minimum(index, width - 1)
            for half in range(2):
                value = None
                for s in range(cycle):
                    piece = jnp.take_along_axis(
                        z[s * rows:(s + 1) * rows, half * width:(half + 1) * width],
                        index, axis=1, mode="promise_in_bounds",
                    )
                    value = piece if value is None else jnp.where(residue == s, piece, value)
                for p in range(part):
                    scaled = value[p * radii:(p + 1) * radii] * scale[p]
                    for g in range(groups):
                        stage[c, owner * groups + g, half, p] = scaled[
                            g * radii_dev:(g + 1) * radii_dev, :mode_dev
                        ]
        field = first // lat_dev
        target = out_ref.at[:, field, pl.ds(time, part)]
        pltpu.make_async_copy(stage.at[c, me], target, out_sem).start()

        @pl.loop(1, everyone)
        def _(i):
            peer = lax.rem(me + i, everyone)
            pltpu.make_async_remote_copy(
                src_ref=stage.at[c, peer],
                dst_ref=target,
                send_sem=stage_sem,
                recv_sem=out_sem,
                device_id={"lon": peer // groups, "lat": lax.rem(peer, groups)},
                device_id_type=MESH,
            ).start()

        return carry

    lax.fori_loop(0, chunks, chunk, 0)

    sent = x_ref.at[pl.ds(0, (cycle - 1) * rows_dev)]
    pltpu.make_async_copy(sent, sent, send_sem).wait()
    for c in range(chunks):
        staged = stage.at[c, pl.ds(0, everyone - 1)]
        pltpu.make_async_copy(staged, staged, stage_sem).wait()
    pltpu.make_async_copy(out_ref, out_ref, out_sem).wait()


def split(both_ref, real_ref, imag_ref, sem):
    copies = [
        pltpu.make_async_copy(both_ref.at[i, f], ref.at[f], sem.at[i, f])
        for i, ref in enumerate((real_ref, imag_ref)) for f in range(ref.shape[0])
    ]
    for copy in copies:
        copy.start()
    for copy in copies:
        copy.wait()


def per_device(grid_field, lat_weight):
    fields, lat_dev, radii, lon_dev = grid_field.shape
    cycle, groups = lax.axis_size("lon"), lax.axis_size("lat")
    mode_dev = MODES // cycle
    width = -(-mode_dev // LANES) * LANES
    rows_dev = fields * lat_dev // cycle
    part = max(1, rows_dev // CHUNKS)
    chunks = rows_dev // part
    rows = part * radii
    twiddle, dft = tables(cycle, lon_dev, width)
    out = pl.pallas_call(
        functools.partial(kernel, cycle, groups, chunks, part, lat_dev, mode_dev),
        out_shape=pltpu.VMEM(
            (2, fields, lat_dev * groups, radii // groups, mode_dev), jnp.float32
        ),
        in_specs=[
            pl.BlockSpec(memory_space=pl.ANY),
            pl.BlockSpec(memory_space=pl.ANY),
            pl.BlockSpec(memory_space=pl.ANY),
            pl.BlockSpec(memory_space=pl.ANY),
        ],
        out_specs=pl.BlockSpec(memory_space=pltpu.VMEM),
        scratch_shapes=[
            pltpu.VMEM((chunks, cycle, part, radii, lon_dev), jnp.float32),
            pltpu.VMEM((chunks, cycle * groups, 2, part, radii // groups, mode_dev), jnp.float32),
            pltpu.VMEM(twiddle.shape, jnp.float32),
            pltpu.VMEM(dft.shape, jnp.bfloat16),
            pltpu.VMEM((cycle * rows, 2 * lon_dev), jnp.bfloat16),
            pltpu.VMEM((cycle * rows, 2 * lon_dev), jnp.bfloat16),
            pltpu.SMEM(lat_weight.shape, jnp.float32),
            pltpu.SemaphoreType.REGULAR((cycle // 2 + groups // 2 - 1,)),
            pltpu.SemaphoreType.DMA((3,)),
            pltpu.SemaphoreType.DMA,
            pltpu.SemaphoreType.DMA((chunks,)),
            pltpu.SemaphoreType.DMA,
            pltpu.SemaphoreType.DMA,
        ],
        compiler_params=pltpu.CompilerParams(collective_id=0, has_side_effects=True, vmem_limit_bytes=67_043_328 - 5 * 2**18),
    )(
        grid_field.reshape(fields * lat_dev, radii, lon_dev), lat_weight,
        jnp.asarray(twiddle), jnp.asarray(dft),
    )
    half = jax.ShapeDtypeStruct(out.shape[1:], jnp.float32)
    return pl.pallas_call(
        split,
        out_shape=(half, half),
        in_specs=[pl.BlockSpec(memory_space=pltpu.VMEM)],
        out_specs=(pl.BlockSpec(memory_space=pl.ANY), pl.BlockSpec(memory_space=pl.ANY)),
        scratch_shapes=[pltpu.SemaphoreType.DMA((2, fields))],
        compiler_params=pltpu.CompilerParams(vmem_limit_bytes=16 * 2**20),
    )(out)


def solution(mesh):
    in_specs = (P(None, "lat", None, "lon"), P())
    out_specs = (P(None, None, "lat", "lon"), P(None, None, "lat", "lon"))
    return jax.shard_map(
        per_device, mesh=mesh, in_specs=in_specs, out_specs=out_specs, check_vma=False
    )
```
